32 devices in a mesh: rep: 2 (over y), tile: 4 (over z), pen: 2 (over x), sub: 2 (over core).
Axes of the slice: x: 2, y: 2, z: 4, core: 2. Of those that a mesh axis runs over, the one named last changes fastest.
Arguments:
- positions: float32 [6, 4, 2, 512], P('rep', 'tile', 'pen'), parts along dimension 0, may hold values from 0 to 256, as said below
- velocities: float32 [6, 4, 2, 512], P('rep', 'tile', 'pen'), parts along dimension 0, may hold values from -5 to 5
- charges: float32 [8, 2, 512], P(('rep', 'tile'), 'pen'), parts along dimension 0, may hold values from -3 to 3
- inverse_mass: float32 [8, 2, 512], P(('rep', 'tile'), 'pen'), parts along dimension 0, may hold values from 0.06 to 1
- export_rows: int32 [8, 2, 128], P(('rep', 'tile'), 'pen'), parts along dimension 0, may hold values from 0 to 511, as said below
- partners: int32 [8, 2, 64, 512], P(('rep', 'tile'), 'pen', 'sub'), parts along dimension 0, may hold values from 0 to 1663, as said below
- bond_partners: int32 [8, 2, 4, 512], P(('rep', 'tile'), 'pen', 'sub'), parts along dimension 0, may hold values from 0 to 511, as said below
- bond_rest: float32 [8, 2, 4, 512], P(('rep', 'tile'), 'pen', 'sub'), parts along dimension 0, may hold values from 1 to 8
- block_offsets: int32 [6, 4, 2, 512], P('rep', 'tile', 'pen'), parts along dimension 0, may hold values from -1 to 254, as said below
Outputs:
- final_positions: float32 [6, 4, 2, 512], P('rep', 'tile', 'pen'), parts along dimension 0
- final_velocities: float32 [6, 4, 2, 512], P('rep', 'tile', 'pen'), parts along dimension 0
- potential: float32 [8, 2, 512], P(('rep', 'tile'), 'pen', 'sub'), parts along dimension 0
The draws below stay inside these ranges and needn't reach their ends.
There are 2 independent parts, one for each index of `rep`. The reference program is written for one: setup_inputs(seed, part) draws one part's arguments, and reference() takes and returns one part's arrays. A program takes and returns all parts, laid end to end along the dimension named above; each array names one. Nothing has to cross between parts.
Inputs may be any that keep to these rules, and one draw needn't show every extreme that they name: `positions`: coordinates of an atom lie strictly between its block offset + 1 and its block offset + 2, coordinate by coordinate. `block_offsets`: for the patch (t, p), x offsets lie in t * 64 - 1 to t * 64 + 62 and y offsets in p * 128 - 1 to p * 128 + 126; z offsets lie in -1 to 254. `export_rows`: rows of the patch's own atoms. `partners`: columns of the patch's table; columns 1024 to 1151 are never named. Slots that an atom does not use name the atom itself. `bond_partners`: rows of the patch's own atoms.
All inputs are finite; a program needn't handle non-finite values.
Results may differ from the reference program's by a relative error of at most 0.0005.
Values sent between devices are 32-bit elements; how exact they have to be, the bound alone decides.
No kernel may reach another device: no remote copies, remote signals or barrier semaphores. Data moves between devices by JAX's collectives and lax.ppermute only.
A program may use at most 128 MiB of HBM per device.

```python
import math
import jax
import jax.numpy as jnp
from jax import lax

GRID = 256
ATOMS = 512
NEIGH = 32
BONDS = 2
INNER = 4
EXPORT = 128
N_TILE = 4
N_PEN = 2


def atom_layout(key):
    keys = jax.random.split(jax.random.fold_in(key, 17), 4)
    shape = (N_TILE, N_PEN, ATOMS)
    planes_x = GRID // N_TILE
    rows_y = GRID // N_PEN
    tiles = jnp.arange(N_TILE, dtype=jnp.int32)[:, None, None]
    pens = jnp.arange(N_PEN, dtype=jnp.int32)[None, :, None]
    atoms = jnp.arange(ATOMS, dtype=jnp.int32)[None, None, :]
    offset_x = tiles * planes_x - 1 + jax.random.randint(keys[0], shape, 0, planes_x)
    offset_y = pens * rows_y - 1 + jax.random.randint(keys[1], shape, 0, rows_y)
    offset_z = jnp.clip(atoms * GRID // ATOMS + jax.random.randint(keys[2], shape, -2, 3), -1, GRID - 2)
    offsets = jnp.stack([offset_x, offset_y, jnp.broadcast_to(offset_z, shape)]).astype(jnp.int32)
    return (offsets, keys[3])


def draw_positions(key, part):
    offsets, frac_key = atom_layout(key)
    frac = jnp.clip(0.5 + 0.18 * jax.random.normal(frac_key, offsets.shape, jnp.float32), 0.05, 0.95)
    return offsets.astype(jnp.float32) + 1.0 + frac


def draw_block_offsets(key, part):
    offsets, frac_key = atom_layout(key)
    return offsets


def draw_export_rows(key, part):
    drawn = jax.random.fold_in(key, 23)
    stride = ATOMS // EXPORT
    rows = jnp.arange(EXPORT, dtype=jnp.int32)[None, None, :] * stride
    return (rows + jax.random.randint(drawn, (N_TILE, N_PEN, EXPORT), 0, stride)).astype(jnp.int32)


def draw_partners(key, part):
    keys = jax.random.split(jax.random.fold_in(key, 29), 5)
    shape = (N_TILE, N_PEN, 2 * NEIGH, ATOMS)
    atoms = jnp.arange(ATOMS, dtype=jnp.int32)[None, None, None, :]
    reach = max(1, 6 * ATOMS // GRID)
    near = jnp.clip(atoms + jax.random.randint(keys[0], shape, -reach, reach + 1), 0, ATOMS - 1)
    neighbour = jax.random.randint(keys[1], shape, 0, 8)
    neighbour = jnp.where(neighbour >= 4, neighbour + 1, neighbour)
    spread = max(1, 6 * EXPORT // GRID)
    column = jnp.clip(atoms * EXPORT // ATOMS + jax.random.randint(keys[2], shape, -spread, spread + 1), 0, EXPORT - 1)
    distant = ATOMS + neighbour * EXPORT + column
    picked = jnp.where(jax.random.randint(keys[3], shape, 0, 2) == 0, near, distant)
    live = jax.random.randint(keys[4], (N_TILE, N_PEN, 1, ATOMS), NEIGH // 2, 2 * NEIGH + 1)
    slots = jnp.arange(2 * NEIGH, dtype=jnp.int32)[None, None, :, None]
    return jnp.where(slots < live, picked, atoms).astype(jnp.int32)


def draw_bond_partners(key, part):
    keys = jax.random.split(jax.random.fold_in(key, 31), 2)
    shape = (N_TILE, N_PEN, 2 * BONDS, ATOMS)
    atoms = jnp.arange(ATOMS, dtype=jnp.int32)[None, None, None, :]
    length = jax.random.randint(keys[0], shape, 1, 4)
    upward = jax.random.randint(keys[1], shape, 0, 2) * 2 - 1
    return jnp.clip(atoms + length * upward, 0, ATOMS - 1).astype(jnp.int32)


def block_levels(stream_key, shape, cuts, smallest, largest):
    def one(dim, parts):
        steps = jax.random.uniform(jax.random.fold_in(jax.random.fold_in(stream_key, 6), dim), (parts,), jnp.float32, smallest / len(cuts), largest / len(cuts))
        return jnp.repeat(jnp.exp(steps), shape[dim] // parts).reshape((-1,) + (1,) * (len(shape) - dim - 1))

    loudness = one(*cuts[0])
    for cut in cuts[1:]:
        loudness = loudness * one(*cut)
    return loudness


def normal_values(stream_key, shape, width, limit, shards=(), kind=jnp.bfloat16):
    factor_of = block_levels(stream_key, shape, shards, -0.22, 0.18) if shards else 1.0
    entries = jax.random.normal(stream_key, shape, jnp.float32) * width * factor_of
    return jnp.minimum(jnp.maximum(entries, -limit), limit).astype(kind)


def setup_inputs(seed: int = 0, part: int = 0) -> dict:
    seeds = jax.random.split(jax.random.key(seed), 10)
    part_keys = jax.random.split(jax.random.fold_in(seeds[9], part), 10)
    return {
        "positions": draw_positions(jax.random.fold_in(jax.random.fold_in(seeds[9], part), 71), part),
        "velocities": normal_values(part_keys[1], (3, N_TILE, N_PEN, ATOMS), 1.0, 5.0, ((1, 4), (2, 2)), jnp.float32),
        "charges": normal_values(part_keys[2], (N_TILE, N_PEN, ATOMS), 0.5, 3.0, ((0, 4), (1, 2)), jnp.float32),
        "inverse_mass": jnp.clip(jnp.exp(math.log(1.0) - 2.8134107 * jax.random.uniform(part_keys[3], (N_TILE, N_PEN, ATOMS), jnp.float32) ** block_levels(part_keys[3], (N_TILE, N_PEN, ATOMS), ((0, 4), (1, 2)), -0.2, 0.2)), 0.06, 1.0),
        "export_rows": draw_export_rows(jax.random.fold_in(jax.random.fold_in(seeds[9], part), 71), part),
        "partners": draw_partners(jax.random.fold_in(jax.random.fold_in(seeds[9], part), 71), part),
        "bond_partners": draw_bond_partners(jax.random.fold_in(jax.random.fold_in(seeds[9], part), 71), part),
        "bond_rest": jnp.clip(1.0 + 7.0 * jax.random.uniform(part_keys[7], (N_TILE, N_PEN, 2 * BONDS, ATOMS), jnp.float32) ** block_levels(part_keys[7], (N_TILE, N_PEN, 2 * BONDS, ATOMS), ((0, 4), (1, 2), (2, 2)), -0.2, 0.2), 1.0, 8.0),
        "block_offsets": draw_block_offsets(jax.random.fold_in(jax.random.fold_in(seeds[9], part), 71), part),
    }


time_step = 0.1
coulomb = 30.0
bond_stiffness = 0.2
soften = 1.0
cutoff_sq = 144.0
ewald_beta = 0.32
highest = lax.Precision.HIGHEST

def spline_pieces(frac):
    rest = 1.0 - frac
    cube = frac * frac * frac
    square = frac * frac
    return (rest * rest * rest / 6.0, (3.0 * cube - 6.0 * square + 4.0) / 6.0, (-3.0 * cube + 3.0 * square + 3.0 * frac + 1.0) / 6.0, cube / 6.0)

def axis_weights(cells, offset, frac, wrapped):
    place = cells[:, None] - offset[None, :]
    if wrapped:
        place = jnp.mod(place, GRID)
    pieces = spline_pieces(frac)
    total = jnp.zeros(place.shape, frac.dtype)
    for order in range(4):
        total = total + jnp.where(place == order, pieces[order][None, :], 0.0)
    return total

def patch_weights(place, offsets, tile_index, pen_index, planes_x, rows_y):
    frac = place - (offsets.astype(place.dtype) + 1.0)
    cells_x = tile_index * planes_x - 1 + jnp.arange(planes_x + 3, dtype=jnp.int32)
    cells_y = pen_index * rows_y - 1 + jnp.arange(rows_y + 3, dtype=jnp.int32)
    weight_x = axis_weights(cells_x, offsets[0], frac[0], False)
    weight_y = axis_weights(cells_y, offsets[1], frac[1], False)
    depth = axis_weights(jnp.arange(GRID, dtype=jnp.int32), offsets[2], frac[2], True)
    plane = (weight_x[:, None, :] * weight_y[None, :, :]).reshape(-1, place.shape[1])
    return (plane, depth)

def influence(freq_x, freq_y, freq_z):

    def signed(freq):
        return jnp.where(freq > GRID // 2, freq - GRID, freq).astype(jnp.float32)

    def modulus(freq):
        angle = 2.0 * math.pi / GRID * freq.astype(jnp.float32)
        real = (1.0 + 4.0 * jnp.cos(angle) + jnp.cos(2.0 * angle)) / 6.0
        imag = (4.0 * jnp.sin(angle) + jnp.sin(2.0 * angle)) / 6.0
        return 1.0 / (real * real + imag * imag)
    sx, sy, sz = (signed(freq_x), signed(freq_y), signed(freq_z))
    m_sq = (sx[:, None, None] ** 2 + sy[None, :, None] ** 2 + sz[None, None, :] ** 2) / float(GRID * GRID)
    anchor = (freq_x[:, None, None] == 0) & (freq_y[None, :, None] == 0) & (freq_z[None, None, :] == 0)
    safe = jnp.where(anchor, 1.0, m_sq)
    value = jnp.exp(-(math.pi / ewald_beta) ** 2 * safe) / (math.pi * float(GRID) ** 3 * safe)
    value = value * modulus(freq_x)[:, None, None] * modulus(freq_y)[None, :, None] * modulus(freq_z)[None, None, :]
    return jnp.where(anchor, 0.0, value)

def hartley(field, axis):
    spectrum = jnp.fft.fft(field, axis=axis)
    return jnp.real(spectrum) - jnp.imag(spectrum)

def pair_force(table, own, charge, neighbours, bonded, rest):
    near = table[:, neighbours]
    delta = own[:, None, :] - near[:3]
    dist_sq = lax.optimization_barrier(jnp.sum(delta * delta, axis=0))
    taper = jnp.where(dist_sq < cutoff_sq, (1.0 - dist_sq / cutoff_sq) ** 2, 0.0)
    strength = coulomb * charge[None, :] * near[3] * taper * (dist_sq + soften) ** (-1.5)
    force = lax.optimization_barrier(jnp.sum(strength[None] * delta, axis=1))
    bond_delta = own[:, None, :] - table[:3][:, bonded]
    length = jnp.sqrt(lax.optimization_barrier(jnp.sum(bond_delta * bond_delta, axis=0)) + soften)
    pull = -bond_stiffness * (length - rest) / length
    return force + lax.optimization_barrier(jnp.sum(pull[None] * bond_delta, axis=1))

def halo_table(coords, charges, export_rows, tiles, pens):
    index = jnp.broadcast_to(export_rows[None], (3,) + export_rows.shape)
    sent = jnp.take_along_axis(coords, index, axis=3)
    sent_charge = jnp.take_along_axis(charges, export_rows, axis=2)
    stacked = jnp.concatenate([sent, sent_charge[None]], axis=0)
    blocks = []
    for across in range(3):
        near_x = tiles + across - 1
        move_x = jnp.where(near_x < 0, -float(GRID), jnp.where(near_x >= N_TILE, float(GRID), 0.0))
        for along in range(3):
            near_y = pens + along - 1
            move_y = jnp.where(near_y < 0, -float(GRID), jnp.where(near_y >= N_PEN, float(GRID), 0.0))
            moved = jnp.roll(stacked, (1 - across, 1 - along), axis=(1, 2))
            blank = jnp.zeros((N_TILE, N_PEN), jnp.float32)
            offset = jnp.stack([jnp.broadcast_to(move_x[:, None], (N_TILE, N_PEN)), jnp.broadcast_to(move_y[None, :], (N_TILE, N_PEN)), blank, blank])
            blocks.append(moved + offset[..., None].astype(moved.dtype))
    own = jnp.concatenate([coords, charges[None]], axis=0)
    return jnp.concatenate([own] + blocks, axis=3)

def reference(positions, velocities, charges, inverse_mass, export_rows, partners, bond_partners, bond_rest, block_offsets):
    planes_x = GRID // N_TILE
    rows_y = GRID // N_PEN
    patch_count = N_TILE * N_PEN
    tiles = jnp.arange(N_TILE, dtype=jnp.int32)
    pens = jnp.arange(N_PEN, dtype=jnp.int32)
    tile_ids = jnp.repeat(tiles, N_PEN)
    pen_ids = jnp.tile(pens, N_TILE)
    flat_partners = partners.reshape(patch_count, -1, ATOMS)
    flat_bonds = bond_partners.reshape(patch_count, -1, ATOMS)
    flat_rest = bond_rest.reshape(patch_count, -1, ATOMS)
    flat_charge = charges.reshape(patch_count, ATOMS)
    coords, speeds = (positions, velocities)

    def patch_force(item):
        table, own, charge, neighbours, bonded, rest = item
        return pair_force(table, own, charge, neighbours, bonded, rest)
    for step in range(INNER):
        table = halo_table(coords, charges, export_rows, tiles, pens)
        flat_table = jnp.transpose(table, (1, 2, 0, 3)).reshape(patch_count, 4, -1)
        flat_coords = jnp.transpose(coords, (1, 2, 0, 3)).reshape(patch_count, 3, ATOMS)
        force = lax.map(patch_force, (flat_table, flat_coords, flat_charge, flat_partners, flat_bonds, flat_rest))
        force = jnp.transpose(force.reshape(N_TILE, N_PEN, 3, ATOMS), (2, 0, 1, 3))
        speeds = speeds + time_step * inverse_mass[None] * force
        coords = coords + time_step * speeds
    flat_coords = jnp.transpose(coords, (1, 2, 0, 3)).reshape(patch_count, 3, ATOMS)
    flat_offsets = jnp.transpose(block_offsets, (1, 2, 0, 3)).reshape(patch_count, 3, ATOMS)

    def spread_patch(item):
        place, offsets, charge, tile_index, pen_index = item
        plane, depth = patch_weights(place, offsets, tile_index, pen_index, planes_x, rows_y)
        local = jnp.einsum('pa,za->pz', plane * charge[None, :], depth, precision=highest)
        return local.reshape(planes_x + 3, rows_y + 3, GRID)
    blocks = lax.map(spread_patch, (flat_coords, flat_offsets, flat_charge, tile_ids, pen_ids))
    blocks = blocks.reshape(N_TILE, N_PEN, planes_x + 3, rows_y + 3, GRID)
    inner_x = blocks[:, :, 1:planes_x + 1]
    from_above = jnp.roll(blocks[:, :, 0:1], -1, axis=0)
    from_below = jnp.roll(blocks[:, :, planes_x + 1:], 1, axis=0)
    inner_x = inner_x.at[:, :, 0:2].add(from_below).at[:, :, planes_x - 1:].add(from_above)
    from_right = jnp.roll(inner_x[:, :, :, 0:1], -1, axis=1)
    from_left = jnp.roll(inner_x[:, :, :, rows_y + 1:], 1, axis=1)
    core = inner_x[:, :, :, 1:rows_y + 1]
    core = core.at[:, :, :, 0:2].add(from_left).at[:, :, :, rows_y - 1:].add(from_right)
    charge_grid = jnp.transpose(core, (0, 2, 1, 3, 4)).reshape(GRID, GRID, GRID)
    spectrum = hartley(hartley(hartley(charge_grid, 2), 1), 0)
    freq = jnp.arange(GRID, dtype=jnp.int32)
    weighted = spectrum * influence(freq, freq, freq)
    potential_grid = hartley(hartley(hartley(weighted, 0), 1), 2)
    padded = jnp.pad(potential_grid, ((1, 2), (1, 2), (0, 0)), mode='wrap')

    def read_patch(item):
        place, offsets, tile_index, pen_index = item
        plane, depth = patch_weights(place, offsets, tile_index, pen_index, planes_x, rows_y)
        corner = (tile_index * planes_x, pen_index * rows_y, jnp.int32(0))
        block = lax.dynamic_slice(padded, corner, (planes_x + 3, rows_y + 3, GRID))
        values = jnp.dot(block.reshape(-1, GRID), depth, precision=highest)
        return lax.optimization_barrier(jnp.sum(values * plane, axis=0))
    potential = lax.map(read_patch, (flat_coords, flat_offsets, tile_ids, pen_ids))
    return (coords, speeds, potential.reshape(N_TILE, N_PEN, ATOMS))
```

```python
import functools
import math

import jax
import jax.numpy as jnp
import numpy as np
from jax import lax
from jax.experimental import pallas as pl
from jax.experimental.pallas import tpu as pltpu
from jax.sharding import PartitionSpec as P

GRID = 256
INNER = 4
LANES = 128
SUBLANES = 8

time_step = 0.1
coulomb = 30.0
bond_stiffness = 0.2
soften = 1.0
cutoff_sq = 144.0
ewald_beta = 0.32


VMEM = pl.BlockSpec(memory_space=pltpu.VMEM)
SMEM = pl.BlockSpec(memory_space=pltpu.SMEM)


def picked(rows, index):
    return jnp.take_along_axis(rows, index, axis=1, mode="promise_in_bounds")


def wide(row):
    return jnp.broadcast_to(row, (SUBLANES, row.shape[1]))


def step_kernel(
    image_ref,
    index_ref,
    rest_ref,
    shown_ref,
    charge_ref,
    scale_ref,
    offset_ref,
    coords_ref,
    speeds_ref,
    middle_ref,
    left_ref,
    right_ref,
    coords_out,
    speeds_out,
    sent_out,
    table,
    *,
    slots,
    merged,
    last,
):
    atoms = coords_ref.shape[1]
    own_chunks = atoms // LANES
    export_chunks = middle_ref.shape[1] // LANES
    chunks = []
    filled = 0

    def fill(rows):
        nonlocal filled
        for row in rows:
            table[filled] = wide(row)
            filled += 1

    for chunk in range(own_chunks):
        cut = slice(chunk * LANES, (chunk + 1) * LANES)
        chunks.append((filled, (chunk,)))
        fill([coords_ref[r : r + 1, cut] for r in range(3)] + [charge_ref[0:1, cut]])
    lower, upper = [], []
    for across in range(3):
        for along in range(3):
            for part in range(export_chunks):
                chunk = own_chunks + (across * 3 + along) * export_chunks + part
                if across == 1 and along == 1:
                    continue
                if along == 0:
                    lower.append(chunk)
                if along == 2:
                    upper.append(chunk)
                    if merged:
                        continue
                source = (left_ref, middle_ref, right_ref)[along]
                cut = slice(part * LANES, (part + 1) * LANES)
                rows = [source[4 * across + r : 4 * across + r + 1, cut] for r in range(4)]
                rows[0] = rows[0] + image_ref[across]
                if not merged:
                    rows[1] = rows[1] + image_ref[3 + along]
                served = (chunk,)
                if merged and along == 0:
                    served = (chunk, chunk + 2 * export_chunks)
                chunks.append((filled, served))
                fill(rows)

    def for_atoms(chunk, carry):
        cut = pl.ds(pl.multiple_of(chunk * LANES, LANES), LANES)
        own = [wide(coords_ref[r : r + 1, cut]) for r in range(3)]
        strength_own = coulomb * charge_ref[0:1, cut]
        total = [jnp.zeros((SUBLANES, LANES), jnp.float32) for _ in range(3)]
        for group in range(slots // SUBLANES):
            index = index_ref[group * SUBLANES : (group + 1) * SUBLANES, cut]
            lane = jnp.bitwise_and(index, LANES - 1)
            high = jnp.right_shift(index, 7)
            near = [jnp.zeros((SUBLANES, LANES), jnp.float32) for _ in range(4)]
            for first, served in chunks:
                hit = high == served[0]
                for other in served[1:]:
                    hit = jnp.logical_or(hit, high == other)
                near = [
                    jnp.where(hit, picked(table[first + r], lane), near[r]) for r in range(4)
                ]
            if merged:
                is_lower = high == lower[0]
                for other in lower[1:]:
                    is_lower = jnp.logical_or(is_lower, high == other)
                is_upper = high == upper[0]
                for other in upper[1:]:
                    is_upper = jnp.logical_or(is_upper, high == other)
                shift = jnp.where(
                    is_lower, image_ref[3], jnp.where(is_upper, image_ref[5], 0.0)
                )
                near[1] = near[1] + shift
            delta = [own[r] - near[r] for r in range(3)]
            dist_sq = delta[0] * delta[0] + delta[1] * delta[1] + delta[2] * delta[2]
            taper = 1.0 - dist_sq * (1.0 / cutoff_sq)
            taper = jnp.where(dist_sq < cutoff_sq, taper * taper, 0.0)
            inverse = lax.rsqrt(dist_sq + soften)
            strength = near[3] * taper * (inverse * inverse * inverse)
            total = [total[r] + strength * delta[r] for r in range(3)]
        total = [strength_own * total[r] for r in range(3)]
        index = index_ref[slots : slots + SUBLANES, cut]
        lane = jnp.bitwise_and(index, LANES - 1)
        high = jnp.right_shift(index, 7)
        near = [jnp.zeros((SUBLANES, LANES), jnp.float32) for _ in range(3)]
        for own_chunk in range(own_chunks):
            hit = high == own_chunk
            near = [
                jnp.where(hit, picked(table[4 * own_chunk + r], lane), near[r]) for r in range(3)
            ]
        delta = [own[r] - near[r] for r in range(3)]
        length = jnp.sqrt(
            delta[0] * delta[0] + delta[1] * delta[1] + delta[2] * delta[2] + soften
        )
        pull = -bond_stiffness * (length - rest_ref[:, cut]) / length
        total = [total[r] + pull * delta[r] for r in range(3)]
        scale = time_step * scale_ref[0:1, cut]
        for r in range(3):
            force = jnp.sum(total[r], axis=0, keepdims=True)
            speed = speeds_ref[r : r + 1, cut] + scale * force
            place = coords_ref[r : r + 1, cut] + time_step * speed
            speeds_out[r : r + 1, cut] = speed
            coords_out[r : r + 1, cut] = place
            if last:
                offset = offset_ref[r : r + 1, cut].astype(jnp.float32)
                frac = place - (offset + 1.0)
                for copy in range(sent_out.shape[0]):
                    sent_out[copy, r : r + 1, cut] = frac
                    sent_out[copy, 3 + r : 4 + r, cut] = offset
        if last:
            both = jnp.concatenate([charge_ref[0:1, cut]] * 2, axis=0)
            for copy in range(sent_out.shape[0]):
                sent_out[copy, 6:8, cut] = both
        return carry

    lax.fori_loop(0, own_chunks, for_atoms, 0)
    if not last:
        for part in range(export_chunks):
            cut = slice(part * LANES, (part + 1) * LANES)
            index = wide(shown_ref[0:1, cut])
            lane = jnp.bitwise_and(index, LANES - 1)
            high = jnp.right_shift(index, 7)
            for r in range(4):
                source = coords_out if r < 3 else charge_ref
                row = r if r < 3 else 0
                out = jnp.zeros((SUBLANES, LANES), jnp.float32)
                for chunk in range(own_chunks):
                    rows = wide(source[row : row + 1, chunk * LANES : (chunk + 1) * LANES])
                    out = jnp.where(high == chunk, picked(rows, lane), out)
                sent_out[r : r + 1, cut] = out[0:1]


def halves(value):
    high = value.astype(jnp.bfloat16)
    low = (value - high.astype(jnp.float32)).astype(jnp.bfloat16)
    return high, low


def product(left, right, transposed=False):
    dims = (((1,), (1 if transposed else 0,)), ((), ()))
    dot = functools.partial(
        lax.dot_general, dimension_numbers=dims, preferred_element_type=jnp.float32
    )
    return dot(left[0], right[0]) + (dot(left[0], right[1]) + dot(left[1], right[0]))


def spline_pieces(frac):
    rest = 1.0 - frac
    square = frac * frac
    cube = square * frac
    return (
        rest * rest * rest * (1.0 / 6.0),
        (3.0 * cube - 6.0 * square + 4.0) * (1.0 / 6.0),
        (-3.0 * cube + 3.0 * square + 3.0 * frac + 1.0) * (1.0 / 6.0),
        cube * (1.0 / 6.0),
    )


def mesh_kernel(
    first_ref,
    depth_ref,
    data_ref,
    cas_ref,
    high_ref,
    low_ref,
    factor_ref,
    square_ref,
    out_ref,
    planes_ref,
    answer_ref,
    high_y,
    low_y,
    weight_x,
    weight_z,
    high_left,
    low_left,
    values,
    *,
    tiles,
    pens,
    depth,
    padded,
    kept,
):
    atoms = data_ref.shape[2]
    width = pens * atoms
    share = GRID // tiles
    reach = share + 3
    first = first_ref[0]
    table = (high_ref[...], low_ref[...])
    per_row = out_ref.shape[1]

    def prepare(tile, slot):
        data = jnp.concatenate([data_ref[tile * pens + p] for p in range(pens)], axis=1)
        pieces = spline_pieces(data[0:1])
        start = data[3:4] - (tile * share - 1).astype(jnp.float32)
        rows = weight_x.shape[1]
        place = lax.broadcasted_iota(jnp.int32, (rows, width), 0).astype(jnp.float32) - start
        total = jnp.zeros((rows, width), jnp.float32)
        for order in range(4):
            total = jnp.where(place == float(order), pieces[order], total)
        weight_x[slot] = total
        pieces = spline_pieces(data[2:3])
        start = data[5:6].astype(jnp.int32)
        for block in range(padded // SUBLANES):
            row = lax.broadcasted_iota(jnp.int32, (SUBLANES, LANES), 0) + block * SUBLANES
            live = row < depth
            freq = row + first
            for chunk in range(width // LANES):
                cut = slice(chunk * LANES, (chunk + 1) * LANES)
                total = jnp.zeros((SUBLANES, LANES), jnp.float32)
                for order in range(4):
                    index = jnp.bitwise_and(freq * (wide(start[:, cut]) + order), GRID - 1)
                    lane = jnp.bitwise_and(index, LANES - 1)
                    wave = picked(cas_ref[:, 0:LANES], lane)
                    for part in range(1, GRID // LANES):
                        wave = jnp.where(
                            jnp.right_shift(index, 7) == part,
                            picked(cas_ref[:, part * LANES : (part + 1) * LANES], lane),
                            wave,
                        )
                    total = total + pieces[order][:, cut] * wave
                if depth < padded:
                    total = jnp.where(live, total, 0.0)
                weight_z[slot, block * SUBLANES : (block + 1) * SUBLANES, cut] = total
        pieces = spline_pieces(data[1:2])
        start = data[4:5].astype(jnp.int32)
        place = jnp.bitwise_and(
            lax.broadcasted_iota(jnp.int32, (GRID, width), 0) - start, GRID - 1
        )
        total = jnp.zeros((GRID, width), jnp.float32)
        for order in range(4):
            total = jnp.where(place == order, pieces[order], total)
        lines = product(table, halves(total))
        high, low = halves(lines)
        high_y[slot] = high
        low_y[slot] = low
        return data[6:7]

    def spread(tile, carry):
        slot = tile if kept else 0
        charge = prepare(tile, slot)
        charged = charge * weight_z[slot]

        def outer(x, carry):
            block = charged * weight_x[slot, pl.ds(x, 1), :]
            high, low = halves(block)
            rows = pl.ds(pl.multiple_of(x * padded, padded), padded)
            high_left[rows, :] = high
            low_left[rows, :] = low
            return carry

        lax.fori_loop(0, reach, outer, 0)
        part = product(
            (high_left[...], low_left[...]), (high_y[slot], low_y[slot]), transposed=True
        )
        rows = pl.ds(pl.multiple_of(tile * share * padded, padded), reach * padded)
        for half in range(GRID // LANES):
            cut = slice(half * LANES, (half + 1) * LANES)
            planes_ref[half, rows, :] = planes_ref[half, rows, :] + part[:, cut]
        return carry

    planes_ref[...] = jnp.zeros(planes_ref.shape, jnp.float32)
    lax.fori_loop(0, tiles, spread, 0)
    edge = 3 * padded
    planes_ref[:, 0:edge, :] = planes_ref[:, 0:edge, :] + planes_ref[:, GRID * padded :, :]

    def solve(k, carry):
        rows = pl.ds(k, GRID, stride=padded)
        parts = [planes_ref[half, rows, :] for half in range(GRID // LANES)]
        spectrum = product(table, halves(jnp.concatenate(parts, axis=1)))
        square = square_ref[...] + depth_ref[0, k]
        anchor = square == 0.0
        factor = factor_ref[...] * depth_ref[1, k]
        influence = jnp.where(anchor, 0.0, factor / jnp.where(anchor, 1.0, square))
        answer = product(table, halves(spectrum * influence))
        for half in range(GRID // LANES):
            answer_ref[half, rows, :] = answer[:, half * LANES : (half + 1) * LANES]
        return carry

    lax.fori_loop(0, depth, solve, 0)
    if depth < padded:
        blank = jnp.zeros((GRID, LANES), jnp.float32)
        for k in range(depth, padded):
            for half in range(GRID // LANES):
                answer_ref[half, pl.ds(k, GRID, stride=padded), :] = blank
    answer_ref[:, GRID * padded :, :] = answer_ref[:, 0:edge, :]

    def read(tile, carry):
        slot = tile if kept else 0
        if not kept:
            prepare(tile, slot)
        rows = pl.ds(pl.multiple_of(tile * share * padded, padded), reach * padded)
        parts = [answer_ref[half, rows, :] for half in range(GRID // LANES)]
        answer = jnp.concatenate(parts, axis=1)
        values[...] = product(halves(answer), (high_y[slot], low_y[slot]))

        def outer(x, total):
            rows = pl.ds(pl.multiple_of(x * padded, padded), padded)
            return total + values[rows, :] * weight_x[slot, pl.ds(x, 1), :]

        total = lax.fori_loop(0, reach, outer, jnp.zeros((padded, width), jnp.float32))
        potential = jnp.sum(total * weight_z[slot], axis=0, keepdims=True)
        for part in range(width // per_row):
            out_ref[pl.ds(tile * (width // per_row) + part, 1), :] = potential[
                :, part * per_row : (part + 1) * per_row
            ]
        return carry

    lax.fori_loop(0, tiles, read, 0)


def grid_tables():
    freq = np.arange(GRID)
    angle = 2.0 * math.pi / GRID * ((freq[:, None] * freq[None, :]) % GRID)
    table = (np.cos(angle) + np.sin(angle)).astype(np.float32)
    signed = np.where(freq > GRID // 2, freq - GRID, freq).astype(np.float64)
    turn = 2.0 * math.pi / GRID * freq
    real = (1.0 + 4.0 * np.cos(turn) + np.cos(2.0 * turn)) / 6.0
    imag = (4.0 * np.sin(turn) + np.sin(2.0 * turn)) / 6.0
    modulus = 1.0 / (real * real + imag * imag)
    square = signed * signed
    factor = modulus * np.exp(-((math.pi / ewald_beta) ** 2) * square / (GRID * GRID))
    return table, square, factor


def mesh_potential(data, tiles, pens, subs, place):
    atoms = data.shape[2]
    depth = GRID // (tiles * pens * subs)
    padded = -(-depth // 16) * 16
    width = pens * atoms
    share = GRID // tiles
    reach = share + 3
    kept = tiles * width * GRID * 4 <= 8 * 2**20
    held = tiles if kept else 1
    table, square, factor = grid_tables()
    exact = jnp.asarray(table)
    high = exact.astype(jnp.bfloat16)
    low = (exact - high.astype(jnp.float32)).astype(jnp.bfloat16)
    wave = jnp.broadcast_to(exact[1:2], (SUBLANES, GRID))
    factor_xy = jnp.asarray((factor[:, None] * factor[None, :]).astype(np.float32))
    square_xy = jnp.asarray((square[:, None] + square[None, :]).astype(np.float32))
    scale = float(GRID * GRID) / (math.pi * float(GRID) ** 3)
    depth_all = jnp.asarray(np.stack([square, factor * scale]).astype(np.float32))
    first = (place * depth).astype(jnp.int32)
    depth_rows = lax.dynamic_slice_in_dim(depth_all, first, depth, 1)
    rows = (GRID + 3) * padded
    return pl.pallas_call(
        functools.partial(
            mesh_kernel, tiles=tiles, pens=pens, depth=depth, padded=padded, kept=kept
        ),
        out_shape=jax.ShapeDtypeStruct((tiles * pens * subs, atoms // subs), jnp.float32),
        in_specs=[SMEM, SMEM, VMEM, VMEM, VMEM, VMEM, VMEM, VMEM],
        out_specs=VMEM,
        scratch_shapes=[
            pltpu.VMEM((GRID // LANES, rows, LANES), jnp.float32),
            pltpu.VMEM((GRID // LANES, rows, LANES), jnp.float32),
            pltpu.VMEM((held, GRID, width), jnp.bfloat16),
            pltpu.VMEM((held, GRID, width), jnp.bfloat16),
            pltpu.VMEM((held, -(-reach // SUBLANES) * SUBLANES, width), jnp.float32),
            pltpu.VMEM((held, padded, width), jnp.float32),
            pltpu.VMEM((reach * padded, width), jnp.bfloat16),
            pltpu.VMEM((reach * padded, width), jnp.bfloat16),
            pltpu.VMEM((reach * padded, width), jnp.float32),
        ],
        name="mesh",
    )(first[None], depth_rows, data, wave, high, low, factor_xy, square_xy)


def shifted(value, axis, steps):
    count = lax.axis_size(axis)
    return lax.ppermute(value, axis, [(i, (i + steps) % count) for i in range(count)])


def on_device(
    positions,
    velocities,
    charges,
    inverse_mass,
    export_rows,
    partners,
    bond_partners,
    bond_rest,
    block_offsets,
):
    tiles = lax.axis_size("tile")
    pens = lax.axis_size("pen")
    subs = lax.axis_size("sub")
    tile_index = lax.axis_index("tile")
    pen_index = lax.axis_index("pen")
    place = lax.axis_index(("tile", "pen", "sub"))
    coords = positions[:, 0, 0]
    speeds = velocities[:, 0, 0]
    charge = charges[0]
    scale = inverse_mass[0]
    shown = export_rows[0]
    offsets = block_offsets[:, 0, 0]
    atoms = coords.shape[1]
    export = shown.shape[1]
    slots = partners.shape[2] * subs
    bonds = bond_partners.shape[2] * subs

    packed = jnp.concatenate(
        [
            partners[0, 0].astype(jnp.float32),
            bond_partners[0, 0].astype(jnp.float32),
            bond_rest[0, 0],
        ],
        axis=0,
    )
    packs = [packed] + [shifted(packed, "sub", s) for s in range(1, subs)]
    near = partners.shape[2]
    tied = bond_partners.shape[2]
    blank = SUBLANES - bonds
    own_atom = jnp.broadcast_to(jnp.arange(atoms, dtype=jnp.float32), (blank, atoms))
    index = jnp.concatenate(
        [p[:near] for p in packs] + [p[near : near + tied] for p in packs] + [own_atom], axis=0
    ).astype(jnp.int32)
    rest = jnp.concatenate(
        [p[near + tied :] for p in packs] + [jnp.ones((blank, atoms), jnp.float32)], axis=0
    )

    border = jnp.arange(3, dtype=jnp.int32) - 1
    near_x = tile_index + border
    near_y = pen_index + border
    move_x = jnp.where(near_x < 0, -float(GRID), jnp.where(near_x >= tiles, float(GRID), 0.0))
    move_y = jnp.where(near_y < 0, -float(GRID), jnp.where(near_y >= pens, float(GRID), 0.0))
    image = jnp.concatenate([move_x, move_y]).astype(jnp.float32)

    merged = pens == 2
    sent = jnp.concatenate([jnp.take(coords, shown[0], axis=1), jnp.take(charge, shown[0], axis=1)])
    for step in range(INNER):
        last = step == INNER - 1
        middle = jnp.concatenate(
            [shifted(sent, "tile", 1), sent, shifted(sent, "tile", -1)], axis=0
        )
        left = shifted(middle, "pen", 1)
        right = left if merged else shifted(middle, "pen", -1)
        sent_shape = (tiles * pens, 8, atoms) if last else (4, export)
        coords, speeds, sent = pl.pallas_call(
            functools.partial(step_kernel, slots=slots, merged=merged, last=last),
            out_shape=(
                jax.ShapeDtypeStruct(coords.shape, jnp.float32),
                jax.ShapeDtypeStruct(speeds.shape, jnp.float32),
                jax.ShapeDtypeStruct(sent_shape, jnp.float32),
            ),
            in_specs=[SMEM] + [VMEM] * 11,
            out_specs=(VMEM, VMEM, VMEM),
            scratch_shapes=[
                pltpu.VMEM(
                    (4 * (atoms // LANES + 8 * (export // LANES)), SUBLANES, LANES), jnp.float32
                )
            ],
            name="last_step" if last else "step",
        )(
            image, index, rest, shown, charge, scale, offsets, coords, speeds, middle, left, right
        )
    data = lax.all_to_all(sent, ("tile", "pen"), 0, 0, tiled=True)
    shares = mesh_potential(data, tiles, pens, subs, place)
    shares = lax.all_to_all(shares, ("tile", "pen", "sub"), 0, 0, tiled=True)
    potential = jnp.sum(shares, axis=0)
    return (coords[:, None, None, :], speeds[:, None, None, :], potential[None, None, :])


def solution(mesh):
    placed = (
        P("rep", "tile", "pen", None),
        P("rep", "tile", "pen", None),
        P(("rep", "tile"), "pen", None),
        P(("rep", "tile"), "pen", None),
        P(("rep", "tile"), "pen", None),
        P(("rep", "tile"), "pen", "sub", None),
        P(("rep", "tile"), "pen", "sub", None),
        P(("rep", "tile"), "pen", "sub", None),
        P("rep", "tile", "pen", None),
    )
    return jax.shard_map(
        on_device,
        mesh=mesh,
        in_specs=placed,
        out_specs=(
            P("rep", "tile", "pen", None),
            P("rep", "tile", "pen", None),
            P(("rep", "tile"), "pen", "sub"),
        ),
        check_vma=False,
    )
```

```python
import functools
import math

import jax
import jax.numpy as jnp
import numpy as np
from jax import lax
from jax.experimental import pallas as pl
from jax.experimental.pallas import tpu as pltpu
from jax.sharding import PartitionSpec as P

GRID = 256
INNER = 4
LANES = 128
SUBLANES = 8

time_step = 0.1
coulomb = 30.0
bond_stiffness = 0.2
soften = 1.0
cutoff_sq = 144.0
ewald_beta = 0.32


VMEM = pl.BlockSpec(memory_space=pltpu.VMEM)
SMEM = pl.BlockSpec(memory_space=pltpu.SMEM)
HBM = pl.BlockSpec(memory_space=pltpu.HBM)


def picked(rows, index):
    return jnp.take_along_axis(rows, index, axis=1, mode="promise_in_bounds")


def wide(row):
    return jnp.broadcast_to(row, (SUBLANES, row.shape[1]))


def gathered(rows, index):
    lane = jnp.bitwise_and(index, LANES - 1)
    high = jnp.right_shift(index, 7)
    out = None
    for chunk, row in enumerate(rows):
        found = picked(wide(row), lane)
        out = found if out is None else jnp.where(high == chunk, found, out)
    return out


def chunks_of(row):
    return [row[:, i * LANES : (i + 1) * LANES] for i in range(row.shape[1] // LANES)]


def show(shown_ref, coords_ref, charge_ref, sent_out):
    for part in range(shown_ref.shape[1] // LANES):
        cut = slice(part * LANES, (part + 1) * LANES)
        index = wide(shown_ref[0:1, cut])
        for r in range(4):
            row = coords_ref[r] if r < 3 else charge_ref[...]
            sent_out[r : r + 1, cut] = gathered(chunks_of(row), index)[0:1]


def brought(sources, targets, semaphores):
    copies = [
        pltpu.make_async_copy(source, target, semaphores.at[i])
        for i, (source, target) in enumerate(zip(sources, targets))
    ]
    for copy in copies:
        copy.start()
    return copies


def first_kernel(*refs, count):
    sources, targets = refs[:count], refs[count : 2 * count]
    sent_out, packed_out, semaphores = refs[2 * count :]
    for copy in brought(sources, targets, semaphores):
        copy.wait()
    shown_ref, charge_ref, _, _, near_ref, tied_ref, rest_ref, coords_ref, _ = targets
    show(shown_ref, coords_ref, charge_ref, sent_out)
    near = near_ref.shape[0]
    tied = tied_ref.shape[0]
    packed_out[0:near] = near_ref[...].astype(jnp.float32)
    packed_out[near : near + tied] = tied_ref[...].astype(jnp.float32)
    packed_out[near + tied : near + 2 * tied] = rest_ref[...]


def step_kernel(*refs, subs, merged, last, tiles, pens):
    shown_ref, charge_ref, scale_ref, offset_ref, near_ref, tied_ref, rest_ref = refs[:7]
    refs = refs[7:]
    other_refs, refs = refs[: subs - 1], refs[subs - 1 :]
    coords_ref, speeds_ref = refs[:2]
    middle_refs, left_refs = refs[2:5], refs[5:8]
    right_refs = left_refs if merged else refs[8:11]
    coords_out, speeds_out, sent_out, table = refs[8 if merged else 11 :]
    atoms = coords_ref.shape[2]
    near = near_ref.shape[0]
    tied = tied_ref.shape[0]
    own_chunks = atoms // LANES
    export_chunks = middle_refs[0].shape[1] // LANES
    tile = lax.axis_index("tile")
    pen = lax.axis_index("pen")

    def moved(place, count):
        low = jnp.where(place < 0, -float(GRID), 0.0)
        return jnp.where(place >= count, float(GRID), low)

    image_x = [moved(tile + i - 1, tiles) for i in range(3)]
    image_y = [moved(pen + i - 1, pens) for i in range(3)]
    chunks = []
    filled = 0

    def fill(rows):
        nonlocal filled
        for row in rows:
            table[filled] = wide(row)
            filled += 1

    for chunk in range(own_chunks):
        cut = slice(chunk * LANES, (chunk + 1) * LANES)
        chunks.append((filled, (chunk,)))
        fill([coords_ref[r, :, cut] for r in range(3)] + [charge_ref[0:1, cut]])
    lower, upper = [], []
    for across in range(3):
        for along in range(3):
            for part in range(export_chunks):
                chunk = own_chunks + (across * 3 + along) * export_chunks + part
                if across == 1 and along == 1:
                    continue
                if along == 0:
                    lower.append(chunk)
                if along == 2:
                    upper.append(chunk)
                    if merged:
                        continue
                source = (left_refs, middle_refs, right_refs)[along][across]
                cut = slice(part * LANES, (part + 1) * LANES)
                rows = [source[r : r + 1, cut] for r in range(4)]
                rows[0] = rows[0] + image_x[across]
                if not merged:
                    rows[1] = rows[1] + image_y[along]
                served = (chunk,)
                if merged and along == 0:
                    served = (chunk, chunk + 2 * export_chunks)
                chunks.append((filled, served))
                fill(rows)

    def among(high, numbers):
        hit = high == numbers[0]
        for other in numbers[1:]:
            hit = jnp.logical_or(hit, high == other)
        return hit

    def for_atoms(chunk, carry):
        cut = pl.ds(pl.multiple_of(chunk * LANES, LANES), LANES)
        own = [wide(coords_ref[r, :, cut]) for r in range(3)]
        total = [jnp.zeros((SUBLANES, LANES), jnp.float32) for _ in range(3)]
        indices = []
        for first in range(0, near, SUBLANES):
            indices.append(near_ref[first : first + SUBLANES, cut])
        for other in other_refs:
            for first in range(0, near, SUBLANES):
                indices.append(other[first : first + SUBLANES, cut].astype(jnp.int32))
        for index in indices:
            lane = jnp.bitwise_and(index, LANES - 1)
            high = jnp.right_shift(index, 7)
            found = [jnp.zeros((SUBLANES, LANES), jnp.float32) for _ in range(4)]
            for first, served in chunks:
                hit = among(high, served)
                found = [
                    jnp.where(hit, picked(table[first + r], lane), found[r]) for r in range(4)
                ]
            if merged:
                shift = jnp.where(among(high, upper), image_y[2], 0.0)
                found[1] = found[1] + jnp.where(among(high, lower), image_y[0], shift)
            delta = [own[r] - found[r] for r in range(3)]
            dist_sq = delta[0] * delta[0] + delta[1] * delta[1] + delta[2] * delta[2]
            taper = 1.0 - dist_sq * (1.0 / cutoff_sq)
            taper = jnp.where(dist_sq < cutoff_sq, taper * taper, 0.0)
            inverse = lax.rsqrt(dist_sq + soften)
            strength = found[3] * taper * (inverse * inverse * inverse)
            total = [total[r] + strength * delta[r] for r in range(3)]
        strength = coulomb * charge_ref[0:1, cut]
        total = [strength * total[r] for r in range(3)]
        blank = SUBLANES - subs * tied
        self_index = lax.broadcasted_iota(jnp.int32, (blank, LANES), 1) + chunk * LANES
        rows = [tied_ref[:, cut]]
        rests = [rest_ref[:, cut]]
        for other in other_refs:
            rows.append(other[near : near + tied, cut].astype(jnp.int32))
            rests.append(other[near + tied : near + 2 * tied, cut])
        index = jnp.concatenate(rows + [self_index], axis=0)
        rest = jnp.concatenate(rests + [jnp.ones((blank, LANES), jnp.float32)], axis=0)
        lane = jnp.bitwise_and(index, LANES - 1)
        high = jnp.right_shift(index, 7)
        found = [jnp.zeros((SUBLANES, LANES), jnp.float32) for _ in range(3)]
        for own_chunk in range(own_chunks):
            hit = high == own_chunk
            found = [
                jnp.where(hit, picked(table[4 * own_chunk + r], lane), found[r]) for r in range(3)
            ]
        delta = [own[r] - found[r] for r in range(3)]
        length = jnp.sqrt(
            delta[0] * delta[0] + delta[1] * delta[1] + delta[2] * delta[2] + soften
        )
        pull = -bond_stiffness * (length - rest) / length
        total = [total[r] + pull * delta[r] for r in range(3)]
        scale = time_step * scale_ref[0:1, cut]
        for r in range(3):
            force = jnp.sum(total[r], axis=0, keepdims=True)
            speed = speeds_ref[r, :, cut] + scale * force
            place = coords_ref[r, :, cut] + time_step * speed
            speeds_out[r, :, cut] = speed
            coords_out[r, :, cut] = place
            if last:
                offset = offset_ref[r, :, cut].astype(jnp.float32)
                frac = place - (offset + 1.0)
                for copy in range(sent_out.shape[0]):
                    sent_out[copy, r : r + 1, cut] = frac
                    sent_out[copy, 3 + r : 4 + r, cut] = offset
        if last:
            both = jnp.concatenate([charge_ref[0:1, cut]] * 2, axis=0)
            for copy in range(sent_out.shape[0]):
                sent_out[copy, 6:8, cut] = both
        return carry

    lax.fori_loop(0, own_chunks, for_atoms, 0)
    if not last:
        show(shown_ref, coords_out, charge_ref, sent_out)


def halves(value):
    high = value.astype(jnp.bfloat16)
    low = (value - high.astype(jnp.float32)).astype(jnp.bfloat16)
    return high, low


def spline_pieces(frac):
    rest = 1.0 - frac
    square = frac * frac
    cube = square * frac
    return (
        rest * rest * rest * (1.0 / 6.0),
        (3.0 * cube - 6.0 * square + 4.0) * (1.0 / 6.0),
        (-3.0 * cube + 3.0 * square + 3.0 * frac + 1.0) * (1.0 / 6.0),
        cube * (1.0 / 6.0),
    )


def spread_rows(start, pieces, rows):
    place = lax.broadcasted_iota(jnp.int32, (rows, start.shape[1]), 0)
    place = place.astype(jnp.float32).astype(jnp.bfloat16) - start.astype(jnp.bfloat16)
    high = jnp.zeros(place.shape, jnp.bfloat16)
    low = high
    for order in range(4):
        hit = place == jnp.bfloat16(order)
        piece_high, piece_low = halves(pieces[order])
        high = jnp.where(hit, piece_high, high)
        low = jnp.where(hit, piece_low, low)
    return high, low


def split_product(left, right, transposed=False):
    dims = (((1,), (1 if transposed else 0,)), ((), ()))
    return lax.dot_general(
        jnp.concatenate([left[0], left[1], left[0]], axis=1),
        jnp.concatenate([right[0], right[0], right[1]], axis=1 if transposed else 0),
        dims,
        preferred_element_type=jnp.float32,
    )


def influence_kernel(
    depth_ref, factor_hbm, square_hbm, out_hbm, factor_ref, square_ref, out_ref, semaphores, done
):
    for copy in brought((factor_hbm, square_hbm), (factor_ref, square_ref), semaphores):
        copy.wait()

    def one(k, carry):
        square = square_ref[...] + depth_ref[0, k]
        anchor = square == 0.0
        factor = factor_ref[...] * depth_ref[1, k]
        out_ref[k] = jnp.where(anchor, 0.0, factor / jnp.where(anchor, 1.0, square))
        return carry

    lax.fori_loop(0, out_ref.shape[0], one, 0)
    copy = pltpu.make_async_copy(out_ref, out_hbm, done)
    copy.start()
    copy.wait()


def mesh_kernel(
    first_ref,
    data_ref,
    wave_ref,
    line_high_hbm,
    line_low_hbm,
    table_high_hbm,
    table_low_hbm,
    influence_hbm,
    out_ref,
    line_high_ref,
    line_low_ref,
    table_high_ref,
    table_low_ref,
    influence_ref,
    semaphores,
    planes_ref,
    answer_ref,
    high_y,
    low_y,
    weight_x,
    weight_z,
    high_left,
    low_left,
    *,
    tiles,
    pens,
    depth,
    padded,
    kept,
    group,
):
    atoms = data_ref.shape[2]
    width = pens * atoms
    share = GRID // tiles
    window = weight_x.shape[1]
    extra = planes_ref.shape[1] - GRID
    rows_y = GRID // pens + 3
    rows_y += -rows_y % 16
    first = first_ref[0]
    copies = brought(
        (line_high_hbm, line_low_hbm, table_high_hbm, table_low_hbm, influence_hbm),
        (line_high_ref, line_low_ref, table_high_ref, table_low_ref, influence_ref),
        semaphores,
    )
    per_row = out_ref.shape[2]

    def prepare(tile, slot):
        data = jnp.concatenate([data_ref[tile * pens + p] for p in range(pens)], axis=1)
        pieces = spline_pieces(data[0:1])
        start = data[3:4] - jnp.float32(tile * share - 1)
        place = lax.broadcasted_iota(jnp.int32, (window, width), 0).astype(jnp.float32) - start
        total = jnp.zeros((window, width), jnp.float32)
        for order in range(4):
            total = jnp.where(place == float(order), pieces[order], total)
        weight_x[slot] = total
        pieces = spline_pieces(data[2:3])
        start = data[5:6].astype(jnp.int32)
        for block in range(weight_z.shape[1] // SUBLANES):
            row = lax.broadcasted_iota(jnp.int32, (SUBLANES, LANES), 0) + block * SUBLANES
            freq = row + first
            for chunk in range(width // LANES):
                cut = slice(chunk * LANES, (chunk + 1) * LANES)
                total = jnp.zeros((SUBLANES, LANES), jnp.float32)
                index = freq * wide(start[:, cut])
                for order in range(4):
                    wave = picked(wave_ref[...], jnp.bitwise_and(index, GRID // 2 - 1))
                    piece = pieces[order][:, cut]
                    back = jnp.bitwise_and(index, GRID // 2) != 0
                    total = total + jnp.where(back, -piece, piece) * wave
                    index = index + freq
                if depth < weight_z.shape[1]:
                    total = jnp.where(row < depth, total, 0.0)
                weight_z[slot, block * SUBLANES : (block + 1) * SUBLANES, cut] = total
        for p in range(pens):
            data = data_ref[tile * pens + p]
            cut = slice(p * atoms, (p + 1) * atoms)
            start = data[4:5] - float(p * (GRID // pens) - 1)
            weight = spread_rows(start, spline_pieces(data[1:2]), rows_y)
            if rows_y < GRID:
                blank = jnp.zeros((GRID - rows_y, atoms), jnp.bfloat16)
                weight = [jnp.concatenate([w, blank], axis=0) for w in weight]
            lines = split_product((line_high_ref[p], line_low_ref[p]), weight)
            high_y[slot, :, cut], low_y[slot, :, cut] = halves(lines)

    def build(tile, slot, side):
        charge = jnp.concatenate([data_ref[tile * pens + p, 6:7] for p in range(pens)], axis=1)
        for pair in range(padded // 2):
            block = jnp.concatenate(
                [
                    weight_x[slot] * (charge * weight_z[slot, 2 * pair + k : 2 * pair + k + 1, :])
                    for k in range(2)
                ],
                axis=0,
            )
            rows = slice(2 * pair * window, 2 * (pair + 1) * window)
            high_left[side, rows], low_left[side, rows] = halves(block)

    def contract(tile, slot, side):
        for some in range(padded // group):
            rows = slice(some * group * window, (some + 1) * group * window)
            part = split_product(
                (high_left[side, rows], low_left[side, rows]),
                (high_y[slot], low_y[slot]),
                transposed=True,
            )
            for k in range(group):
                here = pl.ds(pl.multiple_of(tile * share, SUBLANES), window)
                into = (some * group + k, here, slice(None))
                planes_ref[into] = planes_ref[into] + part[k * window : (k + 1) * window]

    planes_ref[...] = jnp.zeros(planes_ref.shape, jnp.float32)
    for copy in copies[:2]:
        copy.wait()
    if kept:
        prepare(0, 0)
        build(0, 0, 0)
        for tile in range(tiles):
            if tile + 1 < tiles:
                prepare(tile + 1, tile + 1)
                build(tile + 1, tile + 1, (tile + 1) % 2)
            contract(tile, tile, tile % 2)
    else:

        def spread(tile, carry):
            prepare(tile, 0)
            build(tile, 0, 0)
            contract(tile, 0, 0)
            return carry

        lax.fori_loop(0, tiles, spread, 0)
    for k in range(padded):
        planes_ref[k, 0:extra] = planes_ref[k, 0:extra] + planes_ref[k, GRID:]
    for copy in copies[2:]:
        copy.wait()
    table = (table_high_ref[...], table_low_ref[...])
    together = math.gcd(depth, 4)

    def solve(some, carry):
        for k in range(together):
            k = some * together + k
            spectrum = split_product(table, halves(planes_ref[k, 0:GRID]))
            answer = split_product(table, halves(spectrum * influence_ref[k]))
            answer_ref[k, 0:GRID] = answer
            answer_ref[k, GRID:] = answer[0:extra]
        return carry

    lax.fori_loop(0, depth // together, solve, 0)
    for k in range(depth, padded):
        answer_ref[k] = jnp.zeros(answer_ref.shape[1:], jnp.float32)

    def read(tile, slot):
        total = jnp.zeros((SUBLANES, width), jnp.float32)
        here = pl.ds(pl.multiple_of(tile * share, SUBLANES), window)
        for some in range(padded // group):
            answer = [answer_ref[some * group + k, here] for k in range(group)]
            value = split_product(
                halves(jnp.concatenate(answer, axis=0)), (high_y[slot], low_y[slot])
            )
            for k in range(group):
                part = value[k * window : (k + 1) * window] * weight_x[slot]
                part = jnp.sum(part.reshape(window // SUBLANES, SUBLANES, width), axis=0)
                row = some * group + k
                total = total + part * weight_z[slot, row : row + 1, :]
        potential = jnp.sum(total, axis=0, keepdims=True)
        for part in range(width // per_row):
            out_ref[tile * (width // per_row) + part] = potential[
                :, part * per_row : (part + 1) * per_row
            ]

    if kept:
        for tile in range(tiles):
            read(tile, tile)
    else:

        def again(tile, carry):
            prepare(tile, 0)
            read(tile, 0)
            return carry

        lax.fori_loop(0, tiles, again, 0)


def cas(product):
    angle = 2.0 * math.pi / GRID * (product % GRID)
    return np.cos(angle) + np.sin(angle)


def table_halves(table):
    exact = jnp.asarray(table.astype(np.float32))
    high = exact.astype(jnp.bfloat16)
    return high, (exact - high.astype(jnp.float32)).astype(jnp.bfloat16)


def grid_factors():
    freq = np.arange(GRID)
    signed = np.where(freq > GRID // 2, freq - GRID, freq).astype(np.float64)
    turn = 2.0 * math.pi / GRID * freq
    real = (1.0 + 4.0 * np.cos(turn) + np.cos(2.0 * turn)) / 6.0
    imag = (4.0 * np.sin(turn) + np.sin(2.0 * turn)) / 6.0
    square = signed * signed
    decay = np.exp(-((math.pi / ewald_beta) ** 2) * square / (GRID * GRID))
    return square, decay / (real * real + imag * imag)


def mesh_influence(place, depth):
    square, factor = grid_factors()
    factor_xy = jnp.asarray((factor[:, None] * factor[None, :]).astype(np.float32))
    square_xy = jnp.asarray((square[:, None] + square[None, :]).astype(np.float32))
    scale = float(GRID * GRID) / (math.pi * float(GRID) ** 3)
    depth_all = jnp.asarray(np.stack([square, factor * scale]).astype(np.float32))
    rows = lax.dynamic_slice_in_dim(depth_all, place * depth, depth, 1)
    return pl.pallas_call(
        influence_kernel,
        out_shape=jax.ShapeDtypeStruct((depth, GRID, GRID), jnp.float32),
        in_specs=[SMEM, HBM, HBM],
        out_specs=HBM,
        scratch_shapes=[
            pltpu.VMEM((GRID, GRID), jnp.float32),
            pltpu.VMEM((GRID, GRID), jnp.float32),
            pltpu.VMEM((depth, GRID, GRID), jnp.float32),
            pltpu.SemaphoreType.DMA((2,)),
            pltpu.SemaphoreType.DMA,
        ],
        cost_estimate=pl.CostEstimate(
            flops=12 * depth * GRID * GRID,
            bytes_accessed=4 * (depth + 2) * GRID * GRID,
            transcendentals=0,
        ),
        compiler_params=pltpu.CompilerParams(vmem_limit_bytes=8 * 2**20),
        name="influence",
    )(
        rows,
        pltpu.with_memory_space_constraint(factor_xy, pltpu.HBM),
        pltpu.with_memory_space_constraint(square_xy, pltpu.HBM),
    )


def mesh_potential(data, influence, tiles, pens, subs, place):
    atoms = data.shape[2]
    depth = influence.shape[0]
    padded = max(depth, 2)
    width = pens * atoms
    share = GRID // tiles
    window = -(-(share + 3) // SUBLANES) * SUBLANES
    kept = tiles * width * GRID * 4 <= 8 * 2**20
    held = tiles if kept else 1
    sides = 2 if kept else 1
    group = min(padded, 8)
    freq = np.arange(GRID)
    table_high, table_low = table_halves(cas(freq[:, None] * freq[None, :]))
    cells = np.arange(pens)[:, None] * (GRID // pens) - 1 + freq[None, :]
    lines = cas(freq[None, :, None] * cells[:, None, :])
    lines = np.where(freq[None, None, :] < GRID // pens + 3, lines, 0.0)
    line_high, line_low = table_halves(lines)
    wave = np.broadcast_to(cas(freq[: GRID // 2])[None], (SUBLANES, GRID // 2))
    plane_rows = GRID + window - share
    deep = -(-padded // SUBLANES) * SUBLANES
    return pl.pallas_call(
        functools.partial(
            mesh_kernel,
            tiles=tiles,
            pens=pens,
            depth=depth,
            padded=padded,
            kept=kept,
            group=group,
        ),
        out_shape=jax.ShapeDtypeStruct((tiles * pens * subs, 1, atoms // subs), jnp.float32),
        in_specs=[SMEM, VMEM, VMEM, HBM, HBM, HBM, HBM, HBM],
        out_specs=VMEM,
        scratch_shapes=[
            pltpu.VMEM(line_high.shape, jnp.bfloat16),
            pltpu.VMEM(line_high.shape, jnp.bfloat16),
            pltpu.VMEM(table_high.shape, jnp.bfloat16),
            pltpu.VMEM(table_high.shape, jnp.bfloat16),
            pltpu.VMEM(influence.shape, jnp.float32),
            pltpu.SemaphoreType.DMA((5,)),
            pltpu.VMEM((padded, plane_rows, GRID), jnp.float32),
            pltpu.VMEM((padded, plane_rows, GRID), jnp.float32),
            pltpu.VMEM((held, GRID, width), jnp.bfloat16),
            pltpu.VMEM((held, GRID, width), jnp.bfloat16),
            pltpu.VMEM((held, window, width), jnp.float32),
            pltpu.VMEM((held, deep, width), jnp.float32),
            pltpu.VMEM((sides, padded * window, width), jnp.bfloat16),
            pltpu.VMEM((sides, padded * window, width), jnp.bfloat16),
        ],
        compiler_params=pltpu.CompilerParams(vmem_limit_bytes=52 * 2**20),
        name="mesh",
    )(
        (place * depth).astype(jnp.int32)[None],
        data,
        jnp.asarray(wave.astype(np.float32)),
        line_high,
        line_low,
        table_high,
        table_low,
        pltpu.with_memory_space_constraint(influence, pltpu.HBM),
    )


def shifted(value, axis, steps):
    count = lax.axis_size(axis)
    return lax.ppermute(value, axis, [(i, (i + steps) % count) for i in range(count)])


def on_device(
    positions,
    velocities,
    charges,
    inverse_mass,
    export_rows,
    partners,
    bond_partners,
    bond_rest,
    block_offsets,
):
    tiles = lax.axis_size("tile")
    pens = lax.axis_size("pen")
    subs = lax.axis_size("sub")
    place = lax.axis_index(("tile", "pen", "sub"))
    coords = positions[:, 0]
    speeds = velocities[:, 0]
    offsets = block_offsets[:, 0]
    charge = charges[0]
    scale = inverse_mass[0]
    shown = export_rows[0]
    near = partners[0, 0]
    tied = bond_partners[0, 0]
    rest = bond_rest[0, 0]
    atoms = coords.shape[2]
    export = shown.shape[1]
    small = pltpu.CompilerParams(vmem_limit_bytes=4 * 2**20)
    inputs = [shown, charge, scale, offsets, near, tied, rest, coords, speeds]
    *inputs, sent, packed = pl.pallas_call(
        functools.partial(first_kernel, count=len(inputs)),
        out_shape=(
            *(jax.ShapeDtypeStruct(value.shape, value.dtype) for value in inputs),
            jax.ShapeDtypeStruct((4, export), jnp.float32),
            jax.ShapeDtypeStruct((near.shape[0] + 2 * tied.shape[0], atoms), jnp.float32),
        ),
        in_specs=[HBM] * len(inputs),
        out_specs=(VMEM,) * (len(inputs) + 2),
        scratch_shapes=[pltpu.SemaphoreType.DMA((len(inputs),))],
        compiler_params=small,
        name="first",
    )(*[pltpu.with_memory_space_constraint(value, pltpu.HBM) for value in inputs])
    *fixed, coords, speeds = inputs
    others = [shifted(packed, "sub", s) for s in range(1, subs)]
    influence = mesh_influence(place, GRID // (tiles * pens * subs))
    merged = pens == 2
    for step in range(INNER):
        last = step == INNER - 1
        middle = [shifted(sent, "tile", 1), sent, shifted(sent, "tile", -1)]
        beside = [shifted(value, "pen", 1) for value in middle]
        if not merged:
            beside += [shifted(value, "pen", -1) for value in middle]
        sent_shape = (tiles * pens, 8, atoms) if last else (4, export)
        operands = [*fixed, *others, coords, speeds]
        operands += middle + beside
        coords, speeds, sent = pl.pallas_call(
            functools.partial(
                step_kernel, subs=subs, merged=merged, last=last, tiles=tiles, pens=pens
            ),
            out_shape=(
                jax.ShapeDtypeStruct(coords.shape, jnp.float32),
                jax.ShapeDtypeStruct(speeds.shape, jnp.float32),
                jax.ShapeDtypeStruct(sent_shape, jnp.float32),
            ),
            in_specs=[VMEM] * len(operands),
            out_specs=(VMEM, VMEM, VMEM),
            scratch_shapes=[
                pltpu.VMEM(
                    (4 * (atoms // LANES + 8 * (export // LANES)), SUBLANES, LANES), jnp.float32
                )
            ],
            compiler_params=small,
            name="last_step" if last else "step",
        )(*operands)
    data = lax.all_to_all(sent, ("tile", "pen"), 0, 0, tiled=True)
    shares = mesh_potential(data, influence, tiles, pens, subs, place)
    shares = lax.all_to_all(shares, ("tile", "pen", "sub"), 0, 0, tiled=True)
    potential = jnp.sum(shares, axis=0)
    return (coords[:, None], speeds[:, None], potential[None])


def solution(mesh):
    placed = (
        P("rep", "tile", "pen", None),
        P("rep", "tile", "pen", None),
        P(("rep", "tile"), "pen", None),
        P(("rep", "tile"), "pen", None),
        P(("rep", "tile"), "pen", None),
        P(("rep", "tile"), "pen", "sub", None),
        P(("rep", "tile"), "pen", "sub", None),
        P(("rep", "tile"), "pen", "sub", None),
        P("rep", "tile", "pen", None),
    )
    return jax.shard_map(
        on_device,
        mesh=mesh,
        in_specs=placed,
        out_specs=(
            P("rep", "tile", "pen", None),
            P("rep", "tile", "pen", None),
            P(("rep", "tile"), "pen", "sub"),
        ),
        check_vma=False,
    )
```
